32 devices in a mesh: px: 8 (over y, x, core), py: 4 (over z).
Axes of the slice: x: 2, y: 2, z: 4, core: 2. Of those that a mesh axis runs over, the one named last changes fastest.
Arguments:
- nodes: bfloat16 [65536, 256], P(('px', 'py')), as said below
- w_query: bfloat16 [256, 256], replicated, may hold values from -0.375 to 0.375
- w_key: bfloat16 [256, 256], replicated, may hold values from -0.375 to 0.375
- w_value: bfloat16 [256, 256], replicated, may hold values from -0.375 to 0.375
- w_out: bfloat16 [256, 256], replicated, may hold values from -0.375 to 0.375
- omega: float32 [4, 64, 64], replicated, may hold values from -6 to 6
- hop_coef: float32 [2, 4], replicated, may hold values from 0.3 to 1
- ln_gain: float32 [256], replicated, may hold values from 0.5 to 1.5
- send_idx: int32 [32, 32, 16], P(('px', 'py')), may hold values from 0 to 2047
- send_count: int32 [32, 32], P(('px', 'py')), may hold values from 0 to 16, as said below
- tile_row: int32 [32, 20], P(('px', 'py')), may hold values from 0 to 15
- tile_col: int32 [32, 20], P(('px', 'py')), may hold values from 0 to 19, each once within a row
- tile_val: bfloat16 [32, 20, 128, 128], P(('px', 'py')), may hold values from -0.5 to 0.5
- grad_out: bfloat16 [65536, 256], P(('px', 'py')), may hold values from -6 to 6
Outputs:
- output: bfloat16 [65536, 256], P(('px', 'py'))
- grad_nodes: bfloat16 [65536, 256], P(('px', 'py'))
The draws below stay inside these ranges and needn't reach their ends.
Inputs may be any that keep to these rules, and one draw needn't show every extreme that they name: `nodes`: node features. `send_idx`: a row of the sending partition's own 2048 nodes. `send_count`: slots at or beyond the count are padding; no partition sends to itself; every partition sends a full block of 16 rows to at least one other. `tile_col`: each partition's list names every column block once.
All inputs are finite; a program needn't handle non-finite values.
Results may differ from the reference program's by a relative error of at most 0.007.
Values may be sent and summed in bfloat16 or wider, within the bound.
A program may use at most 128 MiB of HBM per device.

```python
import jax
import jax.numpy as jnp
from jax import lax

D = 256
H = 4
DH = 64
M = 64
TILE = 128
R = 2048
BND = 16
PEERS = 32
NODES = 65536
NBR = 16
NT = 20


def draw_nodes(key, part):
    first, second = jax.random.split(key, 2)
    base = jax.random.normal(first, (NODES, D), jnp.float32)
    offset = jax.random.uniform(second, (1, D), jnp.float32, -1.0, 1.0)
    return (base + offset).astype(jnp.bfloat16)


def draw_send_count(key, part):
    first, second = jax.random.split(key)
    counts = jax.random.randint(first, (PEERS, PEERS), 0, BND + 1, dtype=jnp.int32)
    shifts = jax.random.randint(second, (PEERS,), 0, PEERS - 1, dtype=jnp.int32)
    ranks = jnp.arange(PEERS, dtype=jnp.int32)
    target = (ranks + 1 + shifts) % PEERS
    counts = jnp.where(ranks[None, :] == target[:, None], BND, counts)
    return jnp.where(ranks[None, :] == ranks[:, None], 0, counts).astype(jnp.int32)


def with_ends(entries, stream_key, smallest, high):
    extent = entries.shape
    index_at = [jax.random.randint(jax.random.fold_in(stream_key, axis), (), 0, extent[axis]) for axis in range(len(extent))]
    entries = entries.at[tuple(index_at)].set(smallest)
    longest = extent.index(max(extent))
    index_at[longest] = (index_at[longest] + 1) % extent[longest]
    return entries.at[tuple(index_at)].set(high)


def shard_levels(own_key, extent, cuts, least, largest):
    gain, own = 1.0, jax.random.fold_in(own_key, 6)
    for position, blocks in cuts:
        heights = jnp.exp(jax.random.uniform(jax.random.fold_in(own, position), (blocks,), jnp.float32, least / len(cuts), largest / len(cuts)))
        gain = gain * jnp.repeat(heights, extent[position] // blocks).reshape([-1 if axis == position else 1 for axis in range(len(extent))])
    return gain


def scatter_about(rng, shape, width, limit, cuts=(), kind=jnp.bfloat16):
    gain = shard_levels(rng, shape, cuts, -0.22, 0.18) if cuts else 1.0
    drawn = jax.random.normal(rng, shape, jnp.float32) * width * gain
    return jnp.minimum(jnp.maximum(drawn, -limit), limit).astype(kind)


def setup_inputs(seed: int = 0) -> dict:
    streams_of = jax.random.split(jax.random.key(seed), 15)
    nodes = draw_nodes(jax.random.fold_in(streams_of[14], 71), 0)
    w_query = scatter_about(streams_of[1], (D, D), D ** -0.5, 0.375)
    w_key = scatter_about(streams_of[2], (D, D), D ** -0.5, 0.375)
    w_value = scatter_about(streams_of[3], (D, D), D ** -0.5, 0.375)
    w_out = scatter_about(streams_of[4], (D, D), D ** -0.5, 0.375)
    omega = scatter_about(streams_of[5], (H, DH, M), 1.0, 6.0, (), jnp.float32)
    hop_coef = jnp.clip(jax.random.uniform(streams_of[6], (2, H), jnp.float32, 0.3, 1.0), 0.3, 1.0)
    ln_gain = jnp.clip(1.0 + 0.1 * jax.random.normal(streams_of[7], (D,), jnp.float32), 0.5, 1.5)
    send_idx = with_ends(jax.random.randint(streams_of[8], (PEERS, PEERS, BND), 0, R), jax.random.fold_in(streams_of[8], 1), 0, R - 1).astype(jnp.int32)
    send_count = draw_send_count(jax.random.fold_in(streams_of[14], 71), 0)
    tile_row = with_ends(jax.random.randint(streams_of[10], (PEERS, NT), 0, NBR), jax.random.fold_in(streams_of[10], 1), 0, NBR - 1).astype(jnp.int32)
    tile_col = jax.vmap(lambda own: jax.random.permutation(own, NT))(jax.random.split(streams_of[11], PEERS)).reshape((PEERS, NT)).astype(jnp.int32)
    tile_val = scatter_about(streams_of[12], (PEERS, NT, TILE, TILE), (TILE * NT // NBR) ** -0.5, 0.5, ((0, 32),))
    grad_out = scatter_about(streams_of[13], (NODES, D), 1.0, 6.0, ((0, 32),))
    return {"nodes": nodes, "w_query": w_query, "w_key": w_key, "w_value": w_value, "w_out": w_out, "omega": omega, "hop_coef": hop_coef, "ln_gain": ln_gain, "send_idx": send_idx, "send_count": send_count, "tile_row": tile_row, "tile_col": tile_col, "tile_val": tile_val, "grad_out": grad_out}


EPSILON = 1e-05
HIGHEST = lax.Precision.HIGHEST

def project(rows_in, w_query, w_key, w_value):
    query = jnp.dot(rows_in, w_query, preferred_element_type=jnp.float32)
    keys = jnp.dot(rows_in, w_key, preferred_element_type=jnp.float32)
    values = jnp.dot(rows_in, w_value, preferred_element_type=jnp.float32)
    return (query, keys, values)

def features(source, omega):
    count = source.shape[0]
    heads = source.reshape(count, H, DH) * DH ** (-0.25)
    lifted = jnp.einsum('nhe,hem->nhm', heads, omega, precision=HIGHEST)
    return jnp.exp(lifted - 0.5 * lax.optimization_barrier(jnp.sum(heads * heads, axis=2, keepdims=True))) * M ** (-0.5)

def key_summary(keys, values, omega):
    lifted = features(keys, omega)
    split_values = values.reshape(values.shape[0], H, DH)
    summary = jnp.einsum('nhm,nhe->hme', lifted, split_values, precision=HIGHEST)
    return (summary, lax.optimization_barrier(jnp.sum(lifted, axis=0)))

def attend(query, summary, normalizer, omega):
    lifted = features(query, omega)
    numerator = jnp.einsum('nhm,hme->nhe', lifted, summary, precision=HIGHEST)
    denominator = jnp.einsum('nhm,hm->nh', lifted, normalizer, precision=HIGHEST)
    return (numerator / denominator[:, :, None]).reshape(query.shape[0], H * DH)

def output_section(rows_in, mixed, w_out):
    total = rows_in.astype(jnp.float32) + jnp.dot(mixed, w_out, preferred_element_type=jnp.float32)
    centred = total - lax.optimization_barrier(jnp.mean(total, axis=1, keepdims=True))
    inverse = lax.rsqrt(lax.optimization_barrier(jnp.mean(centred * centred, axis=1, keepdims=True)) + EPSILON)
    return (centred * inverse, inverse)

def norm_back(grad_rows, normed, inverse, ln_gain):
    scaled = grad_rows.astype(jnp.float32) * ln_gain
    return inverse * (scaled - lax.optimization_barrier(jnp.mean(scaled, axis=1, keepdims=True)) - normed * lax.optimization_barrier(jnp.mean(scaled * normed, axis=1, keepdims=True)))

def spread(extended, tiles, tile_rows, tile_cols):
    blocks = extended.reshape(NT, TILE, D)[tile_cols]
    products = jnp.einsum('tij,tjd->tid', tiles.astype(jnp.float32), blocks.astype(jnp.float32), precision=HIGHEST)
    member = (tile_rows[None, :] == jnp.arange(NBR, dtype=jnp.int32)[:, None]).astype(jnp.float32)
    return jnp.einsum('bt,tid->bid', member, products, precision=HIGHEST).reshape(R, D)

def collect(grads, tiles, tile_rows, tile_cols):
    blocks = grads.reshape(NBR, TILE, D)[tile_rows]
    products = jnp.einsum('tij,tid->tjd', tiles.astype(jnp.float32), blocks.astype(jnp.float32), precision=HIGHEST)
    member = (tile_cols[None, :] == jnp.arange(NT, dtype=jnp.int32)[:, None]).astype(jnp.float32)
    return jnp.einsum('bt,tjd->bjd', member, products, precision=HIGHEST).reshape(NT * TILE, D)

def hop_all(source, send_idx, send_count, tile_row, tile_col, tile_val):
    flat = source.reshape(PEERS * R, D)
    offsets = (jnp.arange(PEERS, dtype=jnp.int32) * R)[:, None]
    slot_ids = jnp.arange(BND, dtype=jnp.int32)[None, :]

    def one(device):
        picked = (send_idx[:, device, :] + offsets).reshape(-1)
        live = (slot_ids < send_count[:, device][:, None]).reshape(-1, 1).astype(source.dtype)
        extended = jnp.concatenate([source[device], flat[picked] * live], axis=0)
        return spread(extended, tile_val[device], tile_row[device], tile_col[device])
    return lax.map(one, jnp.arange(PEERS, dtype=jnp.int32))

def hop_back_all(grads, send_idx, send_count, tile_row, tile_col, tile_val):
    slot_ids = jnp.arange(BND, dtype=jnp.int32)[None, :]

    def first(device):
        backward = collect(grads[device], tile_val[device], tile_row[device], tile_col[device])
        return (backward[:R], backward[R:].astype(jnp.bfloat16).reshape(PEERS, BND, D))
    local_part, remote = lax.map(first, jnp.arange(PEERS, dtype=jnp.int32))

    def second(device):
        parcel = remote[:, device].reshape(PEERS * BND, D).astype(jnp.float32)
        live = (slot_ids < send_count[device][:, None]).reshape(-1, 1).astype(jnp.float32)
        return jnp.zeros((R, D), jnp.float32).at[send_idx[device].reshape(-1)].add(parcel * live)
    returned = lax.map(second, jnp.arange(PEERS, dtype=jnp.int32))
    return local_part + returned

def reference(nodes, w_query, w_key, w_value, w_out, omega, hop_coef, ln_gain, send_idx, send_count, tile_row, tile_col, tile_val, grad_out):
    rows_x = nodes.reshape(PEERS, R, D)
    rows_g = grad_out.reshape(PEERS, R, D)
    every = jnp.arange(PEERS, dtype=jnp.int32)

    def first(device):
        query, keys, values = project(rows_x[device], w_query, w_key, w_value)
        local_summary, local_norm = key_summary(keys, values, omega)
        return (local_summary, local_norm, values.astype(jnp.bfloat16))
    sums_part, norms_part, values_b = lax.map(first, every)
    summary = lax.optimization_barrier(jnp.sum(sums_part, axis=0))
    normalizer = lax.optimization_barrier(jnp.sum(norms_part, axis=0))
    near = hop_all(values_b, send_idx, send_count, tile_row, tile_col, tile_val)
    near_b = near.astype(jnp.bfloat16)
    far = hop_all(near_b, send_idx, send_count, tile_row, tile_col, tile_val)
    hop_scale = jnp.repeat(hop_coef, DH, axis=1)

    def second(device):
        query, keys, values = project(rows_x[device], w_query, w_key, w_value)
        attention, pull = jax.vjp(lambda first_arg, second_arg, third_arg: attend(first_arg, second_arg, third_arg, omega), query, summary, normalizer)
        mixed = (attention + hop_scale[0] * near[device] + hop_scale[1] * far[device]).astype(jnp.bfloat16)
        normed, inverse = output_section(rows_x[device], mixed, w_out)
        output = (normed * ln_gain).astype(jnp.bfloat16)
        grad_total = norm_back(rows_g[device], normed, inverse, ln_gain)
        grad_mixed = jnp.dot(grad_total.astype(jnp.bfloat16), w_out.T, preferred_element_type=jnp.float32)
        grad_query, grad_summary, grad_norm = pull(grad_mixed)
        grad_far = (hop_scale[1] * grad_mixed).astype(jnp.bfloat16)
        return (output, grad_total, grad_mixed, grad_query, grad_summary, grad_norm, grad_far)
    output, grad_total, grad_mixed, grad_query, grad_summary, grad_norm, grad_far = lax.map(second, every)
    summary_total = lax.optimization_barrier(jnp.sum(grad_summary, axis=0))
    norm_total = lax.optimization_barrier(jnp.sum(grad_norm, axis=0))
    grad_near = hop_scale[0] * grad_mixed + hop_back_all(grad_far, send_idx, send_count, tile_row, tile_col, tile_val)
    grad_hop = hop_back_all(grad_near.astype(jnp.bfloat16), send_idx, send_count, tile_row, tile_col, tile_val)

    def third(device):
        query, keys, values = project(rows_x[device], w_query, w_key, w_value)
        _, pull_keys = jax.vjp(lambda first_arg, second_arg: key_summary(first_arg, second_arg, omega), keys, values)
        grad_keys, grad_values = pull_keys((summary_total, norm_total))
        grad_values = grad_values + grad_hop[device]
        grad_nodes = grad_total[device] + jnp.dot(grad_query[device].astype(jnp.bfloat16), w_query.T, preferred_element_type=jnp.float32)
        grad_nodes = grad_nodes + jnp.dot(grad_keys.astype(jnp.bfloat16), w_key.T, preferred_element_type=jnp.float32)
        grad_nodes = grad_nodes + jnp.dot(grad_values.astype(jnp.bfloat16), w_value.T, preferred_element_type=jnp.float32)
        return grad_nodes.astype(jnp.bfloat16)
    grad_nodes = lax.map(third, every)
    return (output.reshape(NODES, D), grad_nodes.reshape(NODES, D))
```

```python
import functools

import jax
import jax.numpy as jnp
from jax import lax
from jax.experimental import pallas as pl
from jax.experimental.pallas import tpu as pltpu
from jax.sharding import PartitionSpec as P

EPSILON = 1e-05
F32 = jnp.float32
BF16 = jnp.bfloat16
EXTRA = 8
BLOCK = 256
NN = (((1,), (0,)), ((), ()))
NT = (((1,), (1,)), ((), ()))
TN = (((0,), (0,)), ((), ()))


def mm(a, b, dims=NN):
    return lax.dot_general(a, b, dims, preferred_element_type=F32)


def split(x):
    high = x.astype(BF16)
    return high, (x - high.astype(F32)).astype(BF16)


def mm3(x, w, dims=NN):
    xh, xl = x
    wh, wl = w
    return mm(xh, wh, dims) + (mm(xl, wh, dims) + mm(xh, wl, dims))


def mm2(x, w, dims=NN):
    xh, xl = x
    return mm(xh, w, dims) + mm(xl, w, dims)


def iota(shape, axis):
    return lax.broadcasted_iota(jnp.int32, shape, axis)


def ones_where(mask):
    return jnp.where(mask, 1.0, 0.0).astype(BF16)


def head_mask(width, head):
    return iota((width, width), 0) // head == iota((width, width), 1) // head


def features(u, omega, ones, head):
    square = mm2(split(u * u), ones)
    return jnp.exp(mm3(split(u), omega) - square * (0.5 * head**-0.5)) * head**-0.5


def features_back(grad, phi, u, omega, ones, head):
    arg = split(grad * phi)
    return mm3(arg, omega, NT) - u * (mm2(arg, ones) * head**-0.5)


def gather_rows(idx_ref, src_ref, pay_ref, slots):
    rows, width = src_ref.shape
    group = 128 // slots

    def step(i, c):
        start = pl.multiple_of(i * 128, 128)
        wanted = idx_ref[pl.ds(start, 128), :]
        picked = mm(ones_where(iota((128, rows), 1) == wanted), src_ref[...])
        pay_ref[pl.ds(i * group, group), 0:slots, :] = picked.astype(BF16).reshape(
            group, slots, width
        )
        return c

    lax.fori_loop(0, idx_ref.shape[0] // 128, step, 0)


def scatter_rows(idx_row, received, start, count):
    slots_all = received.shape[0]
    hit = ones_where(iota((count, slots_all), 0) + start == idx_row)
    return mm(hit, received)


def pack_sums(pay_ref, slots, total, norm, head, per):
    peers, _, width = pay_ref.shape
    kept = jnp.where(head_mask(width, head), total, 0.0)
    folded = kept[0:head]
    for h in range(1, width // head):
        folded = folded + kept[h * head : (h + 1) * head]
    high, low = split(folded)
    nh, nl = split(norm)
    r, m = iota((peers * EXTRA, head), 0), iota((peers * EXTRA, head), 1)
    owner = m // per == r // EXTRA
    slot = r % EXTRA
    out = mm(ones_where(owner & (slot == m % per)), high)
    out = out + mm(ones_where(owner & (slot == m % per + per)), low)
    k = iota((peers * EXTRA, width), 0) % EXTRA
    out = out + jnp.where(k == EXTRA - 2, nh.astype(F32), 0.0)
    out = out + jnp.where(k == EXTRA - 1, nl.astype(F32), 0.0)
    pay_ref[:, slots : slots + EXTRA, :] = out.reshape(peers, EXTRA, width).astype(BF16)


def relay_sums(rec_ref, pay_ref, slots, norm_ref, per):
    peers, _, width = rec_ref.shape
    s8 = jnp.sum(rec_ref[:, slots : slots + EXTRA, :].astype(F32), axis=0)
    norm = s8[EXTRA - 2 : EXTRA - 1] + s8[EXTRA - 1 : EXTRA]
    norm_ref[...] = jnp.broadcast_to(norm, (8, width))
    k = iota((EXTRA, width), 0)
    own = s8 + pltpu.roll(s8, EXTRA - per, 0)
    high = own.astype(BF16).astype(F32)
    low = pltpu.roll(own - high, per, 0)
    out = jnp.where(k < per, high, jnp.where(k < 2 * per, low, 0.0))
    pay_ref[:, slots : slots + EXTRA, :] = jnp.broadcast_to(
        out[None], (peers, EXTRA, width)
    ).astype(BF16)


def unpack_sums(rec_ref, slots, head, per):
    peers, _, width = rec_ref.shape
    sent = rec_ref[:, slots : slots + EXTRA, :].astype(F32).reshape(peers * EXTRA, width)
    sent = sent.astype(BF16)
    m, r = iota((head, peers * EXTRA), 0), iota((head, peers * EXTRA), 1)
    owner = m // per == r // EXTRA
    slot = r % EXTRA
    mask = head_mask(width, head)
    out = []
    for at in (m % per, m % per + per):
        piece = mm(ones_where(owner & (slot == at)), sent)
        full = jnp.concatenate([piece] * (width // head), axis=0)
        out.append(jnp.where(mask, full, 0.0).astype(BF16))
    return tuple(out)


def spread(row_ref, col_ref, tiles_ref, src_ref, rec_ref, slots, out_ref):
    rows, width = src_ref.shape
    tile = tiles_ref.shape[1]
    group = tile // slots
    own = rows // tile
    out_ref[...] = jnp.zeros_like(out_ref)
    peers = rec_ref.shape[0]

    def step(t, c):
        block = col_ref[0, t]
        at = pl.multiple_of(row_ref[0, t] * tile, tile)
        first = pl.multiple_of(jnp.minimum(block, own - 1) * tile, tile)
        far = jnp.clip(block - own, 0, peers // group - 1) * group
        mine = src_ref[pl.ds(first, tile), :]
        theirs = rec_ref[pl.ds(far, group), 0:slots, :].reshape(tile, width)
        picked = jnp.where(block < own, mine, theirs)
        out_ref[pl.ds(at, tile), :] += mm(tiles_ref[t], picked)
        return c

    lax.fori_loop(0, tiles_ref.shape[0], step, 0, unroll=4)


def collect(row_ref, col_ref, tiles_ref, src_ref, pay_ref, slots, local_ref):
    rows, width = src_ref.shape
    tile = tiles_ref.shape[1]
    group = tile // slots
    own = rows // tile

    def step(t, c):
        block = col_ref[0, t]
        at = pl.multiple_of(row_ref[0, t] * tile, tile)
        product = mm(tiles_ref[t], src_ref[pl.ds(at, tile), :], TN)

        @pl.when(block < own)
        def _():
            local_ref[pl.ds(pl.multiple_of(block * tile, tile), tile), :] = product

        @pl.when(block >= own)
        def _():
            pay_ref[pl.ds((block - own) * group, group), 0:slots, :] = product.astype(
                BF16
            ).reshape(group, slots, width)

        return c

    lax.fori_loop(0, tiles_ref.shape[0], step, 0, unroll=4)


def over_blocks(rows, step):
    def run(i, c):
        step(pl.multiple_of(i * BLOCK, BLOCK))
        return c

    lax.fori_loop(0, rows // BLOCK, run, 0)


def first_kernel(dims, idx, nodes, w_key, w_value, omega, values_b, pay, total, norm):
    head, slots, per = dims
    width = nodes.shape[1]
    ones = ones_where(head_mask(width, head))
    om = split(omega[...])
    total[...] = jnp.zeros_like(total)
    norm[...] = jnp.zeros_like(norm)

    def step(at):
        x = nodes[pl.ds(at, BLOCK), :]
        keys = mm(x, w_key[...])
        values = mm(x, w_value[...])
        phi = features(keys, om, ones, head)
        values_b[pl.ds(at, BLOCK), :] = values.astype(BF16)
        total[...] += mm3(split(phi), split(values), TN)
        norm[...] += jnp.sum(phi, axis=0, keepdims=True)

    over_blocks(nodes.shape[0], step)
    gather_rows(idx, values_b, pay, slots)
    pack_sums(pay, slots, total[...], norm[...], head, per)


def second_kernel(dims, row, col, idx, values_b, rec, tiles, near_b, pay, norm, near):
    head, slots, per = dims
    relay_sums(rec, pay, slots, norm, per)
    spread(row, col, tiles, values_b, rec, slots, near)

    def step(at):
        near_b[pl.ds(at, BLOCK), :] = near[pl.ds(at, BLOCK), :].astype(BF16)

    over_blocks(near.shape[0], step)
    gather_rows(idx, near_b, pay, slots)


def third_kernel(
    dims, row, col, coef, nodes, grad_out, near_b, rec, norm, tiles, w_query, w_out, omega, gain,
    output, partial, grad_near, pay, far, grad_far, total, dnorm, local,
):
    head, slots, per = dims
    rows, width = nodes.shape
    ones = ones_where(head_mask(width, head))
    om = split(omega[...])
    summary = unpack_sums(rec, slots, head, per)
    z = norm[0:1, :]
    lane_head = iota((1, width), 1) // head
    near_scale = jnp.zeros((1, width), F32)
    far_scale = jnp.zeros((1, width), F32)
    for h in range(width // head):
        near_scale = jnp.where(lane_head == h, coef[0, h], near_scale)
        far_scale = jnp.where(lane_head == h, coef[1, h], far_scale)
    spread(row, col, tiles, near_b, rec, slots, far)
    total[...] = jnp.zeros_like(total)
    dnorm[...] = jnp.zeros_like(dnorm)

    def step(at):
        here = pl.ds(at, BLOCK)
        x = nodes[here, :]
        query = mm(x, w_query[...])
        phi = features(query, om, ones, head)
        phis = split(phi)
        inv_den = 1.0 / mm2(split(phi * z), ones)
        attention = mm3(phis, summary) * inv_den
        mixed = attention + near_scale * near_b[here, :].astype(F32) + far_scale * far[here, :]
        whole = x.astype(F32) + mm(mixed.astype(BF16), w_out[...])
        centred = whole - jnp.mean(whole, axis=1, keepdims=True)
        inverse = lax.rsqrt(jnp.mean(centred * centred, axis=1, keepdims=True) + EPSILON)
        normed = centred * inverse
        output[here, :] = (normed * gain[...]).astype(BF16)
        g = grad_out[here, :].astype(F32) * gain[...]
        grad_total = inverse * (
            g
            - jnp.mean(g, axis=1, keepdims=True)
            - normed * jnp.mean(g * normed, axis=1, keepdims=True)
        )
        grad_mixed = mm(grad_total.astype(BF16), w_out[...], NT)
        grad_far[here, :] = (far_scale * grad_mixed).astype(BF16)
        grad_near[here, :] = near_scale * grad_mixed
        a = grad_mixed * inv_den
        pulls = split(a)
        r = mm2(split(a * attention), ones)
        grad_phi = mm3(pulls, summary, NT) - r * z
        total[...] += mm3(phis, pulls, TN)
        dnorm[...] -= jnp.sum(phi * r, axis=0, keepdims=True)
        grad_query = features_back(grad_phi, phi, query, om, ones, head)
        partial[here, :] = grad_total + mm(grad_query.astype(BF16), w_query[...], NT)

    over_blocks(rows, step)
    collect(row, col, tiles, grad_far, pay, slots, local)

    def add(at):
        here = pl.ds(at, BLOCK)
        grad_near[here, :] += local[here, :]

    over_blocks(rows, add)
    pack_sums(pay, slots, total[...], dnorm[...], head, per)


def fourth_kernel(dims, row, col, idx_row, grad_near, rec, tiles, grad_hop, pay, norm, near_b):
    head, slots, per = dims
    peers, _, width = rec.shape
    relay_sums(rec, pay, slots, norm, per)
    returned = rec[:, 0:slots, :].reshape(peers * slots, width)
    wanted = idx_row[...]

    def step(at):
        here = pl.ds(at, BLOCK)
        added = scatter_rows(wanted, returned, at, BLOCK)
        near_b[here, :] = (grad_near[here, :] + added).astype(BF16)

    over_blocks(near_b.shape[0], step)
    collect(row, col, tiles, near_b, pay, slots, grad_hop)


def fifth_kernel(
    dims, idx_row, nodes, partial, grad_hop, rec, norm, w_key, w_value, omega, grad_nodes
):
    head, slots, per = dims
    peers, _, width = rec.shape
    ones = ones_where(head_mask(width, head))
    om = split(omega[...])
    summary = unpack_sums(rec, slots, head, per)
    z = norm[0:1, :]
    returned = rec[:, 0:slots, :].reshape(peers * slots, width)
    wanted = idx_row[...]

    def step(at):
        here = pl.ds(at, BLOCK)
        x = nodes[here, :]
        keys = mm(x, w_key[...])
        values = mm(x, w_value[...])
        phi = features(keys, om, ones, head)
        grad_phi = mm3(split(values), summary, NT) + z
        added = scatter_rows(wanted, returned, at, BLOCK)
        grad_values = mm3(split(phi), summary) + (grad_hop[here, :] + added)
        grad_keys = features_back(grad_phi, phi, keys, om, ones, head)
        out = partial[here, :] + mm(grad_keys.astype(BF16), w_key[...], NT)
        out = out + mm(grad_values.astype(BF16), w_value[...], NT)
        grad_nodes[here, :] = out.astype(BF16)

    over_blocks(nodes.shape[0], step)


def call(body, dims, name, smem, outs, scratch, *args):
    vm = pl.BlockSpec(memory_space=pltpu.VMEM)
    sm = pl.BlockSpec(memory_space=pltpu.SMEM)
    return pl.pallas_call(
        functools.partial(body, dims),
        in_specs=[sm] * smem + [vm] * (len(args) - smem),
        out_specs=[vm] * len(outs),
        out_shape=[jax.ShapeDtypeStruct(s, t) for s, t in outs],
        scratch_shapes=[pltpu.VMEM(s, t) for s, t in scratch],
        name=name,
    )(*args)


def exchange(parcel):
    return lax.all_to_all(parcel, ("px", "py"), split_axis=0, concat_axis=0, tiled=True)


def shards(
    nodes, w_query, w_key, w_value, w_out, omega, hop_coef, ln_gain,
    send_idx, send_count, tile_row, tile_col, tile_val, grad_out,
):
    rows, width = nodes.shape
    heads, head, _ = omega.shape
    tiles = tile_val[0]
    peers, slots = send_idx.shape[1:]
    per = -(-head // peers)
    assert 2 * per <= EXTRA - 2
    dims = (head, slots, per)
    live = jnp.arange(slots, dtype=jnp.int32)[None, :] < send_count[0][:, None]
    idx = jnp.where(live, send_idx[0], -1)
    idx_row = idx.reshape(1, peers * slots)
    idx_col = idx.reshape(peers * slots, 1)
    lane = jnp.arange(width, dtype=jnp.int32) // head
    wide = jnp.tile(omega.reshape(width, head), (1, heads)) * head**-0.25
    wide = jnp.where(lane[:, None] == lane[None, :], wide, 0.0)
    gain = ln_gain.reshape(1, width)
    full_b, full_f = ((rows, width), BF16), ((rows, width), F32)
    pay = ((peers, slots + EXTRA, width), BF16)
    norm = ((8, width), F32)
    sums, row = ((width, width), F32), ((1, width), F32)

    values_b, sent = call(
        first_kernel, dims, "keys", 0, [full_b, pay], [sums, row],
        idx_col, nodes, w_key, w_value, wide,
    )
    got = exchange(sent)
    near_b, sent, z = call(
        second_kernel, dims, "near", 2, [full_b, pay, norm], [full_f],
        tile_row, tile_col, idx_col, values_b, got, tiles,
    )
    got = exchange(sent)
    output, partial, grad_near, sent = call(
        third_kernel, dims, "middle", 3, [full_b, full_f, full_f, pay],
        [full_f, full_b, sums, row, full_f],
        tile_row, tile_col, hop_coef, nodes, grad_out, near_b, got, z, tiles,
        w_query, w_out, wide, gain,
    )
    got = exchange(sent)
    grad_hop, sent, dz = call(
        fourth_kernel, dims, "back", 2, [full_f, pay, norm], [full_b],
        tile_row, tile_col, idx_row, grad_near, got, tiles,
    )
    got = exchange(sent)
    (grad_nodes,) = call(
        fifth_kernel, dims, "last", 0, [full_b], [],
        idx_row, nodes, partial, grad_hop, got, dz, w_key, w_value, wide,
    )
    return output, grad_nodes


def solution(mesh):
    both = ("px", "py")
    in_specs = (
        P(both, None), P(), P(), P(), P(), P(), P(), P(),
        P(both, None, None), P(both, None), P(both, None), P(both, None),
        P(both, None, None, None), P(both, None),
    )
    out_specs = (P(both, None), P(both, None))
    return jax.shard_map(shards, mesh=mesh, in_specs=in_specs, out_specs=out_specs, check_vma=False)
```
